32 devices in a mesh: group: 1, expert: 16 (over z, y, x), step: 2 (over core).
Axes of the slice: x: 2, y: 2, z: 4, core: 2. Of those that a mesh axis runs over, the one named last changes fastest.
Arguments:
- latents: float32 [2, 2048, 1536], P('step', ('group', 'expert')), may hold values from -6 to 6
- modulation: float32 [2, 6, 1536], P('group'), may hold values from -3 to 3
- shallow_routes: int32 [2, 2048, 2], P('step', ('group', 'expert')), may hold values from 0 to 3, all different within a row; in each aligned block of 128 rows (0 to 127, 128 to 255, ..., all dimensions but the last counted through in order) at most 64 rows name the same one
- deep_routes: int32 [2048, 2], P(('group', 'expert')), may hold values from 0 to 3, all different within a row; in each aligned block of 128 rows (0 to 127, 128 to 255, ...) at most 64 rows name the same one
- refresh: int32 [16], P(('group', 'expert')), may hold values from 0 to 1
- shallow_in: bfloat16 [16, 1536, 768], P('expert'), may hold values from -0.15625 to 0.15625
- shallow_out: bfloat16 [16, 768, 1536], P('expert'), may hold values from -0.109375 to 0.109375
- deep_in: bfloat16 [16, 1536, 768], P('expert'), may hold values from -0.15625 to 0.15625
- deep_out: bfloat16 [16, 768, 1536], P('expert'), may hold values from -0.109375 to 0.109375
- shallow_router: float32 [1536, 4], replicated, may hold values from -0.15625 to 0.15625
- deep_router: float32 [1536, 4], replicated, may hold values from -0.15625 to 0.15625
Outputs:
- result: bfloat16 [2, 2048, 1536], P('step', ('group', 'expert'))
The draws below stay inside these ranges and needn't reach their ends.
Inputs may be any that keep to these rules, and one draw needn't show every extreme that they name: `shallow_routes`: within the 128 rows of one index of expert (aligned blocks), each expert is named by at most 64 rows, and by exactly 64 rows in some block; a row names two different experts. `deep_routes`: within the 128 rows of one index of expert (aligned blocks), each expert is named by at most 64 rows, and by exactly 64 rows in some block; a row names two different experts.
All inputs are finite; a program needn't handle non-finite values.
Results may differ from the reference program's by a relative error of at most 0.01.
Values may be sent and summed in bfloat16 or wider, within the bound.
No kernel may reach another device: no remote copies, remote signals or barrier semaphores. Data moves between devices by JAX's collectives and lax.ppermute only.
A program may use at most 64 MiB of HBM per device.

```python
import math
import jax
import jax.numpy as jnp
import numpy as np
from jax import lax

D = 1536
FF = 3072
QUARTERS = 4
TOK_DEV = 128
EXPERTS = 4
FF_DEV = 768
CAP = 64
TOKENS = 2048
N_EXPERT = 16


def with_ends(result, rng, smallest, largest):
    place = [jax.random.randint(jax.random.fold_in(rng, axis), (), 0, length) for axis, length in enumerate(result.shape)]
    main_axis = result.shape.index(max(result.shape))
    beside = place[:main_axis] + [(place[main_axis] + 1) % result.shape[main_axis]] + place[main_axis + 1:]
    return result.at[tuple(place)].set(smallest).at[tuple(beside)].set(largest)


def block_levels(rng, shape, shards, low, largest):
    factor_of = 1.0
    for dim, parts in shards:
        steps = jax.random.uniform(jax.random.fold_in(jax.random.fold_in(rng, 6), dim), (parts,), jnp.float32, low / len(shards), largest / len(shards))
        factor_of = factor_of * jnp.repeat(jnp.exp(steps), shape[dim] // parts).reshape((-1,) + (1,) * (len(shape) - 1 - dim))
    return factor_of


def routed_block(own_key, own, number, rows, amount, top, reach, lean):
    sequence = jax.random.permutation(own_key, amount)
    heavy_load, ordinary = shares(amount, rows * top, reach, lean, True), shares(amount, rows * top, reach, lean, False)
    places = jnp.arange(amount)

    def named(tallies, rotation):
        used = int((tallies > 0).sum())
        fixed = max(1, used // 4)
        shifted = fixed + (places - fixed + rotation * (used - fixed)) % max(1, amount - fixed)
        return jnp.zeros((amount,), jnp.int32).at[sequence[jnp.where(places < fixed, places, shifted)]].set(jnp.asarray(tallies, jnp.int32))

    tallies = jnp.where(number % 4 == 0, named(heavy_load, number // 4), named(ordinary, number - number // 4 - 1))
    mixed = jax.random.permutation(jax.random.fold_in(own, 3), amount)
    donor, receiver = mixed[0:amount // 2 * 2:2], mixed[1:amount // 2 * 2:2]
    slack = jnp.minimum(tallies[donor] - 1, reach - tallies[receiver]) // 2
    slack = jnp.where((donor == sequence[0]) | (receiver == sequence[0]) | (tallies[receiver] == 0), 0, jnp.maximum(slack, 0))
    shifted = jax.random.randint(jax.random.fold_in(own, 4), (amount // 2,), 0, 1 << 20) % (slack + 1)
    tallies = tallies.at[donor].add(-shifted).at[receiver].add(shifted)
    members = jnp.searchsorted(jnp.cumsum(tallies), jnp.arange(rows * top), side="right").astype(jnp.int32)
    listing = members.reshape(top, rows).T
    listing = listing[jax.random.permutation(jax.random.fold_in(own, 1), rows)]
    rotation = jax.random.randint(jax.random.fold_in(own, 2), (rows, 1), 0, top)
    return jnp.take_along_axis(listing, (jnp.arange(top)[None, :] + rotation) % top, axis=1)


def shares(count, total, most, slope, full):
    loads = [(1 << 20) // math.isqrt(rank ** slope) + 1 for rank in range(1, count + 1)]
    largest = most if full else min(most, max(-(-total // count), total * loads[0] // sum(loads)))
    least = 1 if total - largest >= count - 1 else 0
    given, rest = [largest] + [least] * (count - 1), total - largest - least * (count - 1)
    while rest > 0:
        candidates = [i for i in range(1, count) if given[i] < largest] or [i for i in range(1, count) if given[i] < most]
        mass, left = sum([loads[i] for i in candidates]), rest
        for i in candidates:
            extra = min(most - given[i], max(1, left * loads[i] // mass), rest)
            given[i] = given[i] + extra
            rest = rest - extra
    return np.array(given)


def bell_draw(stream_key, shape, deviation, most, pieces=(), held_as=jnp.bfloat16):
    entries = jax.random.normal(stream_key, shape, jnp.float32) * deviation
    if len(pieces) > 0:
        entries = block_levels(stream_key, shape, pieces, -0.22, 0.18) * entries
    return jnp.clip(entries, min=-most, max=most).astype(held_as)


def setup_inputs(seed: int = 0, part: int = 0) -> dict:
    seeds = jax.random.split(jax.random.key(seed), 12)
    part_keys = jax.random.split(jax.random.fold_in(seeds[11], part), 12)
    latents = bell_draw(part_keys[0], (2, TOKENS, D), 1.0, 6.0, ((0, 2), (1, 16)), jnp.float32)
    modulation = bell_draw(part_keys[1], (2, 6, D), 0.5, 3.0, (), jnp.float32)
    shallow_routes_keys = jax.random.split(jax.random.fold_in(part_keys[2], 1), 2 * TOKENS // TOK_DEV)
    shallow_routes_turns = jax.random.permutation(jax.random.fold_in(part_keys[2], 3), 2 * TOKENS // TOK_DEV)
    shallow_routes = jax.vmap(lambda own, number: routed_block(jax.random.fold_in(part_keys[2], 2), own, number, TOK_DEV, EXPERTS, 2, CAP, 1))(shallow_routes_keys, shallow_routes_turns).reshape((2, TOKENS, 2))
    deep_routes_keys = jax.random.split(jax.random.fold_in(part_keys[3], 1), TOKENS // TOK_DEV)
    deep_routes_turns = jax.random.permutation(jax.random.fold_in(part_keys[3], 3), TOKENS // TOK_DEV)
    deep_routes = jax.vmap(lambda own, number: routed_block(jax.random.fold_in(part_keys[3], 2), own, number, TOK_DEV, EXPERTS, 2, CAP, 1))(deep_routes_keys, deep_routes_turns).reshape((TOKENS, 2))
    refresh = with_ends(jax.random.randint(part_keys[4], (N_EXPERT,), 0, 2), jax.random.fold_in(part_keys[4], 1), 0, 1).astype(jnp.int32)
    shallow_in = bell_draw(seeds[5], (N_EXPERT, D, FF_DEV), D ** -0.5, 0.15625, ((0, 16),))
    shallow_out = bell_draw(seeds[6], (N_EXPERT, FF_DEV, D), FF ** -0.5, 0.109375, ((0, 16),))
    deep_in = bell_draw(seeds[7], (N_EXPERT, D, FF_DEV), D ** -0.5, 0.15625, ((0, 16),))
    deep_out = bell_draw(seeds[8], (N_EXPERT, FF_DEV, D), FF ** -0.5, 0.109375, ((0, 16),))
    shallow_router = bell_draw(seeds[9], (D, EXPERTS), D ** -0.5, 0.15625, (), jnp.float32)
    deep_router = bell_draw(seeds[10], (D, EXPERTS), D ** -0.5, 0.15625, (), jnp.float32)
    return {"latents": latents, "modulation": modulation, "shallow_routes": shallow_routes, "deep_routes": deep_routes, "refresh": refresh, "shallow_in": shallow_in, "shallow_out": shallow_out, "deep_in": deep_in, "deep_out": deep_out, "shallow_router": shallow_router, "deep_router": deep_router}


def modulate(hidden, shift_row, scale_row):
    average = lax.optimization_barrier(jnp.mean(hidden, axis=-1, keepdims=True))
    centred = hidden - average
    variance = lax.optimization_barrier(jnp.mean(centred * centred, axis=-1, keepdims=True))
    return (centred * lax.rsqrt(variance + 1e-06) * (1.0 + scale_row) + shift_row).astype(jnp.bfloat16)

def expert_layer(normed, routes, weight_in, weight_out, router):
    total = normed.shape[0]
    blocks = total // TOK_DEV
    logits = jnp.dot(normed.astype(jnp.float32), router, precision=lax.Precision.HIGHEST)
    chosen = jnp.take_along_axis(logits, routes, axis=1)
    gate_sig = jax.nn.sigmoid(chosen)
    weights = gate_sig / lax.optimization_barrier(jnp.sum(gate_sig, axis=-1, keepdims=True))
    pair_expert = routes.reshape(blocks, TOK_DEV * 2).astype(jnp.int32)
    onehot = (pair_expert[:, :, None] == jnp.arange(EXPERTS, dtype=jnp.int32)).astype(jnp.int32)
    position = lax.optimization_barrier(jnp.sum(onehot * (jnp.cumsum(onehot, axis=1) - 1), axis=-1)).astype(jnp.int32)
    block_ids = jnp.broadcast_to(jnp.arange(blocks, dtype=jnp.int32)[:, None], position.shape)
    token_ids = (jnp.arange(total * 2, dtype=jnp.int32) // 2).reshape(blocks, TOK_DEV * 2)
    slot_table = jnp.full((EXPERTS, blocks, CAP), total, jnp.int32).at[pair_expert, block_ids, position].set(token_ids)
    padded = jnp.concatenate([normed, jnp.zeros((1, D), jnp.bfloat16)], axis=0)

    def one_expert(expert):
        flat_rows = padded[slot_table[expert].reshape(-1)]
        summed = jnp.zeros((blocks * CAP, D), jnp.float32)
        for quarter in range(QUARTERS):
            index = expert * QUARTERS + quarter
            hidden = jax.nn.gelu(jnp.dot(flat_rows, weight_in[index], preferred_element_type=jnp.float32), approximate=True).astype(jnp.bfloat16)
            partial_value = lax.optimization_barrier(jnp.dot(hidden, weight_out[index], preferred_element_type=jnp.float32).astype(jnp.bfloat16))
            summed = summed + partial_value.astype(jnp.float32)
        return summed
    expert_out = lax.map(one_expert, jnp.arange(EXPERTS, dtype=jnp.int32))
    picked = expert_out[pair_expert, block_ids * CAP + position].reshape(total, 2, D)
    return lax.optimization_barrier(jnp.sum(weights[:, :, None] * picked, axis=1))

def reference(latents, modulation, shallow_routes, deep_routes, refresh, shallow_in, shallow_out, deep_in, deep_out, shallow_router, deep_router):
    shallow = []
    for group_idx in range(2):
        normed = modulate(latents[group_idx], modulation[group_idx, 0], modulation[group_idx, 1])
        moe_out = expert_layer(normed, shallow_routes[group_idx], shallow_in, shallow_out, shallow_router)
        shallow.append((latents[group_idx] + modulation[group_idx, 2] * moe_out).astype(jnp.bfloat16))
    after_shallow = jnp.stack(shallow)
    token_root = jnp.repeat(refresh.astype(jnp.int32), TOK_DEV)
    picks_one = (token_root == 1)[:, None]
    chosen_rows = jnp.where(picks_one, after_shallow[1], after_shallow[0])

    def mod_row(index):
        return jnp.where(picks_one, modulation[1, index][None], modulation[0, index][None])
    normed = modulate(chosen_rows.astype(jnp.float32), mod_row(3), mod_row(4))
    moe_out = expert_layer(normed, deep_routes, deep_in, deep_out, deep_router)
    deep_delta = (mod_row(5) * moe_out).astype(jnp.bfloat16)
    return (after_shallow.astype(jnp.float32) + deep_delta.astype(jnp.float32)[None]).astype(jnp.bfloat16)
```

```python
import functools

import jax
import jax.numpy as jnp
from jax import lax
from jax.experimental import pallas as pl
from jax.experimental.pallas import tpu as pltpu
from jax.sharding import PartitionSpec as P

BF = jnp.bfloat16
F32 = jnp.float32
VMEM = pltpu.VMEM
SMEM = pltpu.SMEM


def pieces3(value):
    high = value.astype(BF)
    rest = value - high.astype(F32)
    middle = rest.astype(BF)
    low = (rest - middle.astype(F32)).astype(BF)
    return high, middle, low


def normalise(hidden, shift_row, scale_row):
    average = jnp.mean(hidden, axis=-1, keepdims=True)
    centred = hidden - average
    variance = jnp.mean(centred * centred, axis=-1, keepdims=True)
    return (centred * lax.rsqrt(variance + 1e-06) * (1.0 + scale_row) + shift_row).astype(BF)


def slot_rows(routes, weights, home, core, experts, half):
    padded = max(8, experts)
    tokens = routes.shape[1]
    relative = routes ^ home
    number = lax.broadcasted_iota(jnp.int32, (padded, tokens), 0)
    first, second = number == relative[0:1], number == relative[1:2]
    hits = first | second
    before = lax.broadcasted_iota(jnp.int32, (tokens, tokens), 0) < lax.broadcasted_iota(
        jnp.int32, (tokens, tokens), 1
    )
    ones = jnp.where(hits, 1.0, 0.0).astype(BF)
    place = jnp.dot(ones, jnp.where(before, 1.0, 0.0).astype(BF), preferred_element_type=F32)
    columns = [jnp.where(hits, place, -1.0).astype(BF)]
    if weights is not None:
        per_expert = jnp.where(first, weights[0:1], jnp.where(second, weights[1:2], 0.0))
        columns.extend(pieces3(per_expert))
    table = jnp.concatenate(columns, axis=1)
    rows = 2 * experts * half
    slot = lax.broadcasted_iota(jnp.int32, (rows, padded), 0)
    block = jnp.where(slot >= experts * half, slot - experts * half, slot)
    owner = lax.broadcasted_iota(jnp.int32, (rows, padded), 1)
    spread = (block >= owner * half) & (block < (owner + 1) * half)
    wide = jnp.dot(jnp.where(spread, 1.0, 0.0).astype(BF), table, preferred_element_type=F32)
    slot = lax.broadcasted_iota(jnp.int32, (rows, tokens), 0)
    other = slot >= experts * half
    block = jnp.where(other, slot - experts * half, slot)
    within = block
    for step in range(1, experts):
        within = within - jnp.where(block >= step * half, half, 0)
    within = within + jnp.where(other, (1 - core) * half, core * half)
    taken = wide[:, :tokens] == within.astype(F32)
    if weights is None:
        return jnp.where(taken, 1.0, 0.0).astype(BF)
    parts = [
        jnp.where(taken, wide[:, (k + 1) * tokens : (k + 2) * tokens], 0.0).astype(BF)
        for k in range(3)
    ]
    return jnp.concatenate(parts, axis=1)


def gate_pack(normed, routes, router_t, experts):
    tokens = normed.shape[0]
    stacked = jnp.concatenate(pieces3(router_t), axis=0)
    logits3 = lax.dot_general(
        stacked, normed, (((1,), (1,)), ((), ())), preferred_element_type=F32
    )
    count = router_t.shape[0]
    logits = logits3[:count] + logits3[count : 2 * count] + logits3[2 * count :]
    number = lax.broadcasted_iota(jnp.int32, (count, tokens), 0)
    gates = []
    for k in range(2):
        chosen = jnp.sum(jnp.where(number == routes[k : k + 1], logits, 0.0), axis=0, keepdims=True)
        gates.append(jax.nn.sigmoid(chosen))
    total = gates[0] + gates[1]
    rows = [gates[0] / total, gates[1] / total, routes.astype(F32), jnp.zeros((4, tokens), F32)]
    return jnp.concatenate(rows, axis=0)


def mixed(rows_ref, pack, home, core, experts, half):
    tokens = pack.shape[1]
    routes = pack[2:4].astype(jnp.int32)
    weighted = slot_rows(routes, pack[0:2], home, core, experts, half)
    out3 = lax.dot_general(
        weighted, rows_ref[...], (((0,), (0,)), ((), ())), preferred_element_type=F32
    )
    return out3[:tokens] + out3[tokens : 2 * tokens] + out3[2 * tokens :]


def padded_router(ref, experts):
    value = ref[...]
    if experts < 8:
        value = jnp.concatenate([value, jnp.zeros((8 - experts, value.shape[1]), F32)], axis=0)
    return value


def pre_kernel(experts, half, scal, feats, mod, routes, router_t, keep, send, pack):
    home, core = scal[0], scal[1]
    normed = normalise(feats[...], mod[core, 0:1, :], mod[core, 1:2, :])
    onehot = slot_rows(routes[...], None, home, core, experts, half)
    rows = jnp.dot(onehot, normed, preferred_element_type=F32).astype(BF)
    keep[...] = rows[: experts * half]
    send[...] = rows[experts * half :]
    pack[...] = gate_pack(normed, routes[...], padded_router(router_t, experts), experts)


def gather_blocks(scratch, blocks):
    start = 0
    for block in blocks:
        scratch[start : start + block.shape[0], :] = block[...]
        start += block.shape[0]


def mid_kernel(experts, half, n_blocks, scal, *refs):
    blocks, refs = refs[:n_blocks], refs[n_blocks:]
    feats, feats_o, pack, pack_o, mod, routes, router_t, after, keep, pack_out, scratch = refs
    home, core, root = scal[0], scal[1], scal[2]
    is_root = core == root
    gather_blocks(scratch, blocks)
    moe = mixed(scratch, jnp.where(is_root, pack[...], pack_o[...]), home, core, experts, half)
    features = jnp.where(is_root, feats[...], feats_o[...])
    shallow = (features + mod[root, 2:3, :] * moe).astype(BF)
    after[...] = shallow
    normed = normalise(shallow.astype(F32), mod[root, 3:4, :], mod[root, 4:5, :])
    onehot = slot_rows(routes[...], None, home, core, experts, half)[: experts * half]
    keep[...] = jnp.dot(onehot, normed, preferred_element_type=F32).astype(BF)
    pack_out[...] = gate_pack(normed, routes[...], padded_router(router_t, experts), experts)


def rest_kernel(experts, half, n_blocks, scal, *refs):
    blocks, refs = refs[:n_blocks], refs[n_blocks:]
    feats, feats_o, pack, pack_o, mod, after, scratch = refs
    home, core, root = scal[0], scal[1], scal[2]
    is_root = core == root
    gather_blocks(scratch, blocks)
    moe = mixed(scratch, jnp.where(is_root, pack_o[...], pack[...]), home, core, experts, half)
    features = jnp.where(is_root, feats_o[...], feats[...])
    after[...] = (features + mod[1 - root, 2:3, :] * moe).astype(BF)


def last_kernel(experts, half, n_blocks, scal, *refs):
    blocks, refs = refs[:n_blocks], refs[n_blocks:]
    pack, mod, after_root, after_rest, result, scratch = refs
    home, core, root = scal[0], scal[1], scal[2]
    gather_blocks(scratch, blocks)
    moe = mixed(scratch, pack[...], home, core, experts, half)
    delta = (mod[root, 5:6, :] * moe).astype(BF)
    mine = jnp.where(core == root, after_root[...].astype(F32), after_rest[...].astype(F32))
    result[...] = (mine + delta.astype(F32)).astype(BF)


def expert_kernel(n_blocks, *refs):
    blocks, (w_in, w_out) = refs[:n_blocks], refs[n_blocks : n_blocks + 2]
    outs, scratch = refs[n_blocks + 2 : -1], refs[-1]
    gather_blocks(scratch, blocks)
    hidden = jnp.dot(scratch[...], w_in[...], preferred_element_type=F32)
    hidden = jax.nn.gelu(hidden, approximate=True).astype(BF)
    value = jnp.dot(hidden, w_out[...], preferred_element_type=F32).astype(BF)
    start = 0
    for out in outs:
        out[...] = value[start : start + out.shape[0]]
        start += out.shape[0]


def call(kernel, outs, scratch, args, flops, name):
    specs = [
        pl.BlockSpec(memory_space=SMEM if a.ndim == 1 else VMEM) for a in args
    ]
    nbytes = sum(a.size * a.dtype.itemsize for a in args) + sum(
        o.size * o.dtype.itemsize for o in outs
    )
    return pl.pallas_call(
        kernel,
        out_shape=outs,
        in_specs=specs,
        out_specs=[pl.BlockSpec(memory_space=VMEM)] * len(outs),
        scratch_shapes=scratch,
        compiler_params=pltpu.CompilerParams(vmem_limit_bytes=28 << 20),
        cost_estimate=pl.CostEstimate(flops=flops, bytes_accessed=nbytes, transcendentals=0),
        name=name,
    )(*args)


def struct(shape, dtype):
    return jax.ShapeDtypeStruct(shape, dtype)


class Links:
    def __init__(self, experts, quarters):
        self.experts, self.quarters = experts, quarters

    def plane(self, value, turn):
        quarters = self.quarters
        pairs = [
            (e * quarters + q, e * quarters + (q ^ turn))
            for e in range(self.experts)
            for q in range(quarters)
        ]
        return lax.ppermute(value, "expert", pairs)

    def far(self, value, turn):
        quarters = self.quarters
        pairs = [
            (e * quarters + q, (e ^ turn) * quarters + q)
            for e in range(self.experts)
            for q in range(quarters)
        ]
        return lax.ppermute(value, "expert", pairs)


def swap(value):
    return lax.ppermute(value, "step", [(0, 1), (1, 0)])


def expert_call(blocks, w_in, w_out):
    rows = sum(b.shape[0] for b in blocks)
    width, hidden = w_in.shape
    outs = [struct(b.shape, BF) for b in blocks]
    return call(
        functools.partial(expert_kernel, len(blocks)),
        outs,
        [pltpu.VMEM((rows, width), BF)],
        (*blocks, w_in, w_out),
        4 * rows * width * hidden,
        "expert_rows",
    )


def layer_half(rows, half, w_in, w_out, links, groups):
    experts = links.experts
    arrived = {}
    for turn in range(experts):
        block = rows[turn * half : (turn + 1) * half]
        arrived[turn] = links.far(block, turn) if turn else block
    back = {}
    for group in groups:
        mine = jnp.concatenate([arrived[t] for t in group], axis=0)
        cut = mine.shape[0] // 2
        from_x = links.plane(mine, 1)
        from_y = links.plane(mine, 2)
        diag_a = links.plane(from_x[:cut], 2)
        diag_b = links.plane(from_y[cut:], 1)
        own, px, py, pa, pb = expert_call([mine, from_x, from_y, diag_a, diag_b], w_in, w_out)
        via_y = links.plane(pa, 2)
        via_x = links.plane(pb, 1)
        to_x = jnp.concatenate(
            [(px[:cut].astype(F32) + via_y.astype(F32)).astype(BF), px[cut:]], axis=0
        )
        to_y = jnp.concatenate(
            [py[:cut], (py[cut:].astype(F32) + via_x.astype(F32)).astype(BF)], axis=0
        )
        total = (
            own.astype(F32)
            + links.plane(to_x, 1).astype(F32)
            + links.plane(to_y, 2).astype(F32)
        ).astype(BF)
        for k, turn in enumerate(group):
            block = total[k * half : (k + 1) * half]
            back[turn] = links.far(block, turn) if turn else block
    return [back[t] for t in range(experts)]


def both_cores(blocks, groups):
    other = {}
    for group in groups:
        joined = swap(jnp.concatenate([blocks[t] for t in group], axis=0))
        size = joined.shape[0] // len(group)
        for k, t in enumerate(group):
            other[t] = joined[k * size : (k + 1) * size]
    return blocks + [other[t] for t in range(len(blocks))]


def body(
    latents,
    modulation,
    shallow_routes,
    deep_routes,
    refresh,
    shallow_in,
    shallow_out,
    deep_in,
    deep_out,
    shallow_router,
    deep_router,
):
    slices = lax.axis_size("expert")
    experts = shallow_router.shape[1]
    quarters = slices // experts
    tokens, width = latents.shape[1:]
    half = max(tokens * 5 // 64, tokens // experts)
    links = Links(experts, quarters)
    core = lax.axis_index("step")
    home = lax.axis_index("expert") // quarters
    root = refresh[0]
    scal = jnp.stack([home, core, root]).astype(jnp.int32)
    is_root = core == root
    slots = experts * half
    partial = functools.partial
    cut = experts // 2
    groups = [list(range(cut)), list(range(cut, experts))]

    feats = latents[0]
    keep, send, pack = call(
        partial(pre_kernel, experts, half),
        [struct((slots, width), BF), struct((slots, width), BF), struct((8, tokens), F32)],
        [],
        (scal, feats, modulation, shallow_routes[0].T, shallow_router.T),
        4 * slots * tokens * width,
        "shallow_start",
    )
    got = swap(send)
    rows_root = jnp.where(is_root, keep, got)
    rows_rest = jnp.where(is_root, got, keep)
    pack_o = swap(pack)
    feats_o = swap(feats)
    scratch = [pltpu.VMEM((2 * slots, width), BF)]
    mix_flops = 12 * slots * tokens * width

    back_root = layer_half(rows_root, half, shallow_in[0], shallow_out[0], links, groups)
    blocks = both_cores(back_root, groups)
    after_root, rows_deep, pack_deep = call(
        partial(mid_kernel, experts, half, len(blocks)),
        [struct((tokens, width), BF), struct((slots, width), BF), struct((8, tokens), F32)],
        scratch,
        (scal, *blocks, feats, feats_o, pack, pack_o, modulation, deep_routes.T, deep_router.T),
        mix_flops,
        "shallow_end",
    )
    back_rest = layer_half(rows_rest, half, shallow_in[0], shallow_out[0], links, groups)
    blocks = both_cores(back_rest, groups)
    (after_rest,) = call(
        partial(rest_kernel, experts, half, len(blocks)),
        [struct((tokens, width), BF)],
        scratch,
        (scal, *blocks, feats, feats_o, pack, pack_o, modulation),
        mix_flops,
        "rest_end",
    )
    back_deep = layer_half(rows_deep, half, deep_in[0], deep_out[0], links, groups)
    blocks = both_cores(back_deep, groups)
    (result,) = call(
        partial(last_kernel, experts, half, len(blocks)),
        [struct((tokens, width), BF)],
        scratch,
        (scal, *blocks, pack_deep, modulation, after_root, after_rest),
        mix_flops,
        "deep_end",
    )
    return result[None]


def solution(mesh):
    in_specs = (
        P("step", ("group", "expert"), None),
        P("group", None, None),
        P("step", ("group", "expert"), None),
        P(("group", "expert"), None),
        P(("group", "expert")),
        P("expert", None, None),
        P("expert", None, None),
        P("expert", None, None),
        P("expert", None, None),
        P(),
        P(),
    )
    out_specs = P("step", ("group", "expert"), None)
    return jax.shard_map(body, mesh=mesh, in_specs=in_specs, out_specs=out_specs, check_vma=False)
```

```python
import functools

import jax
import jax.numpy as jnp
from jax import lax
from jax.experimental import pallas as pl
from jax.experimental.pallas import tpu as pltpu
from jax.sharding import PartitionSpec as P

BF = jnp.bfloat16
F32 = jnp.float32
VMEM = pltpu.VMEM
SMEM = pltpu.SMEM


def pieces3(value):
    high = value.astype(BF)
    rest = value - high.astype(F32)
    middle = rest.astype(BF)
    low = (rest - middle.astype(F32)).astype(BF)
    return high, middle, low


def normalise(hidden, shift_row, scale_row):
    average = jnp.mean(hidden, axis=-1, keepdims=True)
    centred = hidden - average
    variance = jnp.mean(centred * centred, axis=-1, keepdims=True)
    return (centred * lax.rsqrt(variance + 1e-06) * (1.0 + scale_row) + shift_row).astype(BF)


def slot_rows(routes, weights, home, core, experts, half):
    padded = max(8, experts)
    tokens = routes.shape[1]
    relative = routes ^ home
    number = lax.broadcasted_iota(jnp.int32, (padded, tokens), 0)
    first, second = number == relative[0:1], number == relative[1:2]
    hits = first | second
    before = lax.broadcasted_iota(jnp.int32, (tokens, tokens), 0) < lax.broadcasted_iota(
        jnp.int32, (tokens, tokens), 1
    )
    ones = jnp.where(hits, 1.0, 0.0).astype(BF)
    place = jnp.dot(ones, jnp.where(before, 1.0, 0.0).astype(BF), preferred_element_type=F32)
    columns = [jnp.where(hits, place, -1.0).astype(BF)]
    if weights is not None:
        per_expert = jnp.where(first, weights[0:1], jnp.where(second, weights[1:2], 0.0))
        columns.extend(pieces3(per_expert))
    table = jnp.concatenate(columns, axis=1)
    rows, mine = 2 * experts * half, experts * half
    slot = lax.broadcasted_iota(jnp.int32, (rows, padded), 0)
    owner = lax.broadcasted_iota(jnp.int32, (rows, padded), 1)
    side = jnp.where(slot >= mine, 1 - core, core)
    block = jnp.where(slot >= mine, slot - mine, slot)
    split = owner < 2
    low = jnp.where(split, owner * half, (owner >> 1) * (2 * half))
    high = low + jnp.where(split, half, 2 * half)
    spread = (block >= low) & (block < high) & (split | ((owner & 1) == side))
    wide = jnp.dot(jnp.where(spread, 1.0, 0.0).astype(BF), table, preferred_element_type=F32)
    slot = lax.broadcasted_iota(jnp.int32, (rows, tokens), 0)
    side = jnp.where(slot >= mine, 1 - core, core)
    block = jnp.where(slot >= mine, slot - mine, slot)
    within = block + jnp.where(block < 2 * half, side * half, 0)
    within = within - jnp.where((block >= half) & (block < 2 * half), half, 0)
    for step in range(1, experts // 2):
        within = within - jnp.where(block >= step * 2 * half, 2 * half, 0)
    taken = wide[:, :tokens] == within.astype(F32)
    if weights is None:
        return jnp.where(taken, 1.0, 0.0).astype(BF)
    parts = [
        jnp.where(taken, wide[:, (k + 1) * tokens : (k + 2) * tokens], 0.0).astype(BF)
        for k in range(3)
    ]
    return jnp.concatenate(parts, axis=1)


def gate_pack(normed, routes, router_t, experts):
    tokens = normed.shape[0]
    stacked = jnp.concatenate(pieces3(router_t), axis=0)
    logits3 = lax.dot_general(
        stacked, normed, (((1,), (1,)), ((), ())), preferred_element_type=F32
    )
    count = router_t.shape[0]
    logits = logits3[:count] + logits3[count : 2 * count] + logits3[2 * count :]
    number = lax.broadcasted_iota(jnp.int32, (count, tokens), 0)
    gates = []
    for k in range(2):
        chosen = jnp.sum(jnp.where(number == routes[k : k + 1], logits, 0.0), axis=0, keepdims=True)
        gates.append(jax.nn.sigmoid(chosen))
    total = gates[0] + gates[1]
    rows = [gates[0] / total, gates[1] / total, routes.astype(F32), jnp.zeros((4, tokens), F32)]
    return jnp.concatenate(rows, axis=0)


def mixed(rows_ref, pack, home, core, experts, half):
    tokens = pack.shape[1]
    routes = pack[2:4].astype(jnp.int32)
    weighted = slot_rows(routes, pack[0:2], home, core, experts, half)
    out3 = lax.dot_general(
        weighted, rows_ref[...], (((0,), (0,)), ((), ())), preferred_element_type=F32
    )
    return out3[:tokens] + out3[tokens : 2 * tokens] + out3[2 * tokens :]


def padded_router(ref, experts):
    value = ref[...]
    if experts < 8:
        value = jnp.concatenate([value, jnp.zeros((8 - experts, value.shape[1]), F32)], axis=0)
    return value


def pre_kernel(experts, half, scal, feats, mod, routes, router_t, keep, send, pack):
    home, core = scal[0], scal[1]
    normed = normalise(feats[...], mod[0, pl.ds(core, 1), :], mod[1, pl.ds(core, 1), :])
    onehot = slot_rows(routes[...], None, home, core, experts, half)
    rows = jnp.dot(onehot, normed, preferred_element_type=F32).astype(BF)
    keep[...] = rows[: experts * half]
    send[...] = rows[experts * half :]
    pack[...] = gate_pack(normed, routes[...], padded_router(router_t, experts), experts)


def gather_blocks(scratch, blocks):
    start = 0
    for block in blocks:
        scratch[start : start + block.shape[0], :] = block[...]
        start += block.shape[0]


def mid_kernel(experts, half, n_blocks, scal, *refs):
    blocks, refs = refs[:n_blocks], refs[n_blocks:]
    feats, feats_o, pack, pack_o, mod, routes, router_t, after, keep, pack_out, scratch = refs
    home, core, root = scal[0], scal[1], scal[2]
    is_root = core == root
    gather_blocks(scratch, blocks)
    moe = mixed(scratch, jnp.where(is_root, pack[...], pack_o[...]), home, core, experts, half)
    features = jnp.where(is_root, feats[...], feats_o[...])
    shallow = (features + mod[2, pl.ds(root, 1), :] * moe).astype(BF)
    after[...] = shallow
    normed = normalise(shallow.astype(F32), mod[3, pl.ds(root, 1), :], mod[4, pl.ds(root, 1), :])
    onehot = slot_rows(routes[...], None, home, core, experts, half)[: experts * half]
    keep[...] = jnp.dot(onehot, normed, preferred_element_type=F32).astype(BF)
    pack_out[...] = gate_pack(normed, routes[...], padded_router(router_t, experts), experts)


def rest_kernel(experts, half, n_blocks, scal, *refs):
    blocks, refs = refs[:n_blocks], refs[n_blocks:]
    feats, feats_o, pack, pack_o, mod, after, scratch = refs
    home, core, root = scal[0], scal[1], scal[2]
    is_root = core == root
    gather_blocks(scratch, blocks)
    moe = mixed(scratch, jnp.where(is_root, pack_o[...], pack[...]), home, core, experts, half)
    features = jnp.where(is_root, feats_o[...], feats[...])
    after[...] = (features + mod[2, pl.ds(1 - root, 1), :] * moe).astype(BF)


def last_kernel(experts, half, n_blocks, scal, *refs):
    blocks, refs = refs[:n_blocks], refs[n_blocks:]
    pack, mod, after_root, after_rest, result, scratch = refs
    home, core, root = scal[0], scal[1], scal[2]
    gather_blocks(scratch, blocks)
    moe = mixed(scratch, pack[...], home, core, experts, half)
    delta = (mod[5, pl.ds(root, 1), :] * moe).astype(BF)
    mine = jnp.where(core == root, after_root[...].astype(F32), after_rest[...].astype(F32))
    result[...] = (mine + delta.astype(F32)).astype(BF)


def expert_kernel(n_blocks, *refs):
    blocks, (w_in, w_out) = refs[:n_blocks], refs[n_blocks : n_blocks + 2]
    outs, scratch = refs[n_blocks + 2 : -1], refs[-1]
    gather_blocks(scratch, blocks)
    hidden = jnp.dot(scratch[...], w_in[...], preferred_element_type=F32)
    hidden = jax.nn.gelu(hidden, approximate=True).astype(BF)
    value = jnp.dot(hidden, w_out[...], preferred_element_type=F32).astype(BF)
    start = 0
    for out in outs:
        out[...] = value[start : start + out.shape[0]]
        start += out.shape[0]


def call(kernel, outs, scratch, args, flops, name):
    specs = [
        pl.BlockSpec(memory_space=SMEM if a.ndim == 1 else VMEM) for a in args
    ]
    nbytes = sum(a.size * a.dtype.itemsize for a in args) + sum(
        o.size * o.dtype.itemsize for o in outs
    )
    return pl.pallas_call(
        kernel,
        out_shape=outs,
        in_specs=specs,
        out_specs=[pl.BlockSpec(memory_space=VMEM)] * len(outs),
        scratch_shapes=scratch,
        compiler_params=pltpu.CompilerParams(vmem_limit_bytes=28 << 20),
        cost_estimate=pl.CostEstimate(flops=flops, bytes_accessed=nbytes, transcendentals=0),
        name=name,
    )(*args)


def struct(shape, dtype):
    return jax.ShapeDtypeStruct(shape, dtype)


class Links:
    def __init__(self, experts, quarters):
        self.experts, self.quarters = experts, quarters

    def send(self, value, turns):
        pairs = []
        for e in range(self.experts):
            for q in range(self.quarters):
                for c, (far, near) in enumerate(turns):
                    target = (e ^ far) * self.quarters + (q ^ near)
                    pairs.append(((e * self.quarters + q) * 2 + c, target * 2 + c))
        return lax.ppermute(value, ("expert", "step"), pairs)

    def first(self, value):
        return self.send(value, ((0, 1), (0, 2)))

    def second(self, value):
        return self.send(value, ((0, 2), (0, 1)))

    def close(self, value):
        return self.send(value, ((1, 0), (1, 0)))

    def far(self, value, pair):
        return self.send(value, ((2 * pair, 0), (2 * pair + 1, 0)))


def swap(value):
    return lax.ppermute(value, "step", [(0, 1), (1, 0)])


def expert_call(blocks, w_in, w_out):
    rows = sum(b.shape[0] for b in blocks)
    width, hidden = w_in.shape
    outs = [struct(b.shape, BF) for b in blocks]
    return call(
        functools.partial(expert_kernel, len(blocks)),
        outs,
        [pltpu.VMEM((rows, width), BF)],
        (*blocks, w_in, w_out),
        4 * rows * width * hidden,
        "expert_rows",
    )


def tie(value, *others):
    return lax.optimization_barrier((value, *others))[0]


def add(*values):
    total = values[0].astype(F32)
    for value in values[1:]:
        total = total + value.astype(F32)
    return total.astype(BF)


class Stage:
    def __init__(self, links, half, w_in, w_out):
        self.links, self.half, self.w_in, self.w_out = links, half, w_in, w_out

    def out_close(self, rows):
        half = self.half
        return jnp.concatenate([rows[:half], self.links.close(rows[half : 2 * half])], axis=0)

    def out_far(self, rows):
        half = self.half
        pairs = self.links.experts // 2
        blocks = [
            self.links.far(rows[2 * half * k : 2 * half * (k + 1)], k) for k in range(1, pairs)
        ]
        return blocks[0] if len(blocks) == 1 else jnp.concatenate(blocks, axis=0)

    def step1(self, chunk):
        return self.links.first(chunk)

    def step2(self, chunk, near):
        return self.links.second(jnp.concatenate([chunk, near], axis=0))

    def experts(self, chunk, near, wide):
        return expert_call([chunk, near, wide], self.w_in, self.w_out)

    def back1(self, wide):
        return self.links.second(wide)

    def back2(self, near, wide):
        size = near.shape[0]
        return self.links.first(add(near, wide[size:]))

    def total(self, own, wide, near):
        return add(own, wide[: own.shape[0]], near)

    def home_close(self, total):
        half = self.half
        return jnp.concatenate([total[:half], self.links.close(total[half:])], axis=0)

    def home_far(self, total):
        half = self.half
        blocks = [
            self.links.far(total[2 * half * k : 2 * half * (k + 1)], k + 1)
            for k in range(total.shape[0] // (2 * half))
        ]
        return blocks[0] if len(blocks) == 1 else jnp.concatenate(blocks, axis=0)


def body(
    latents,
    modulation,
    shallow_routes,
    deep_routes,
    refresh,
    shallow_in,
    shallow_out,
    deep_in,
    deep_out,
    shallow_router,
    deep_router,
):
    slices = lax.axis_size("expert")
    experts = shallow_router.shape[1]
    quarters = slices // experts
    tokens, width = latents.shape[1:]
    half = max(tokens * 5 // 64, tokens // experts)
    links = Links(experts, quarters)
    core = lax.axis_index("step")
    home = lax.axis_index("expert") // quarters
    root = refresh[0]
    scal = jnp.stack([home, core, root]).astype(jnp.int32)
    is_root = core == root
    slots = experts * half
    partial = functools.partial
    feats = latents[0]
    modulation = modulation.transpose(1, 0, 2)
    keep, send, pack = call(
        partial(pre_kernel, experts, half),
        [struct((slots, width), BF), struct((slots, width), BF), struct((8, tokens), F32)],
        [],
        (scal, feats, modulation, shallow_routes[0].T, shallow_router.T),
        4 * slots * tokens * width,
        "shallow_start",
    )
    got = swap(send)
    rows_root = jnp.where(is_root, keep, got)
    rows_rest = jnp.where(is_root, got, keep)
    pack_o = swap(pack)
    feats_o = swap(feats)
    scratch = [pltpu.VMEM((2 * slots, width), BF)]
    mix_flops = 12 * slots * tokens * width

    one = Stage(links, half, shallow_in[0], shallow_out[0])
    two = Stage(links, half, shallow_in[0], shallow_out[0])
    three = Stage(links, half, deep_in[0], deep_out[0])

    a_far = one.out_far(rows_root)
    a_close = one.out_close(rows_root)
    a_near1 = one.step1(a_close)
    a_wide1 = one.step2(a_close, a_near1)
    a_near2 = one.step1(a_far)
    a_wide2 = one.step2(a_far, a_near2)
    b_close = two.out_close(rows_rest)
    b_far = two.out_far(tie(rows_rest, a_far))
    b_close = tie(b_close, a_near1)
    b_near1 = two.step1(b_close)
    b_wide1 = two.step2(b_close, b_near1)
    a_own1, a_n1, a_w1 = one.experts(a_close, a_near1, a_wide1)
    a_own2, a_n2, a_w2 = one.experts(a_far, a_near2, a_wide2)
    a_bw2 = one.back1(a_w2)
    a_bn2 = one.back2(a_n2, a_bw2)
    a_total2 = one.total(a_own2, a_bw2, a_bn2)
    a_home2 = one.home_far(a_total2)
    a_bw1 = one.back1(a_w1)
    a_bn1 = one.back2(a_n1, a_bw1)
    a_home1 = one.home_close(one.total(a_own1, a_bw1, a_bn1))
    b_far = tie(b_far, a_total2)
    b_near2 = two.step1(b_far)
    b_wide2 = two.step2(b_far, b_near2)
    b_own1, b_n1, b_w1 = two.experts(b_close, b_near1, b_wide1)
    b_own2, b_n2, b_w2 = two.experts(b_far, b_near2, b_wide2)
    blocks = [a_home1, a_home2, swap(a_home1), swap(a_home2)]
    after_root, rows_deep, pack_deep = call(
        partial(mid_kernel, experts, half, len(blocks)),
        [struct((tokens, width), BF), struct((slots, width), BF), struct((8, tokens), F32)],
        scratch,
        (scal, *blocks, feats, feats_o, pack, pack_o, modulation, deep_routes.T, deep_router.T),
        mix_flops,
        "shallow_end",
    )
    c_far = three.out_far(rows_deep)
    c_close = three.out_close(rows_deep)
    c_near1 = three.step1(c_close)
    c_wide1 = three.step2(c_close, c_near1)
    c_near2 = three.step1(c_far)
    c_wide2 = three.step2(c_far, c_near2)
    b_bw1 = two.back1(tie(b_w1, a_total2))
    b_bn1 = two.back2(b_n1, b_bw1)
    b_bw2 = two.back1(tie(b_w2, rows_deep))
    b_bn2 = two.back2(b_n2, b_bw2)
    b_home1 = two.home_close(two.total(b_own1, b_bw1, b_bn1))
    b_home2 = two.home_far(tie(two.total(b_own2, b_bw2, b_bn2), c_far))
    blocks = [b_home1, b_home2, swap(b_home1), swap(b_home2)]
    (after_rest,) = call(
        partial(rest_kernel, experts, half, len(blocks)),
        [struct((tokens, width), BF)],
        scratch,
        (scal, *blocks, feats, feats_o, pack, pack_o, modulation),
        mix_flops,
        "rest_end",
    )
    c_own1, c_n1, c_w1 = three.experts(c_close, c_near1, c_wide1)
    c_own2, c_n2, c_w2 = three.experts(c_far, c_near2, c_wide2)
    c_bw2 = three.back1(c_w2)
    c_bn2 = three.back2(c_n2, c_bw2)
    c_home2 = three.home_far(three.total(c_own2, c_bw2, c_bn2))
    c_bw1 = three.back1(c_w1)
    c_bn1 = three.back2(c_n1, c_bw1)
    c_home1 = three.home_close(three.total(c_own1, c_bw1, c_bn1))
    blocks = [c_home1, c_home2, swap(c_home1), swap(c_home2)]
    (result,) = call(
        partial(last_kernel, experts, half, len(blocks)),
        [struct((tokens, width), BF)],
        scratch,
        (scal, *blocks, pack_deep, modulation, after_root, after_rest),
        mix_flops,
        "deep_end",
    )
    return result[None]


def solution(mesh):
    in_specs = (
        P("step", ("group", "expert"), None),
        P("group", None, None),
        P("step", ("group", "expert"), None),
        P(("group", "expert"), None),
        P(("group", "expert")),
        P("expert", None, None),
        P("expert", None, None),
        P("expert", None, None),
        P("expert", None, None),
        P(),
        P(),
    )
    out_specs = P("step", ("group", "expert"), None)
    return jax.shard_map(body, mesh=mesh, in_specs=in_specs, out_specs=out_specs, check_vma=False)
```
